32 devices in a mesh: group: 4 (over z), seq: 8 (over y, x, core).
Axes of the slice: x: 2, y: 2, z: 4, core: 2. Of those that a mesh axis runs over, the one named last changes fastest.
Arguments:
- vis_query: bfloat16 [8, 32, 1280], P('group', 'seq'), parts along dimension 0, may hold values from -200 to 200
- vis_key: bfloat16 [8, 32, 1280], P('group', 'seq'), parts along dimension 0, may hold values from -200 to 200
- vis_value: bfloat16 [8, 32, 1280], P('group', 'seq'), parts along dimension 0, may hold values from -6 to 6
- vis_resid: bfloat16 [8, 32, 1280], P('group', 'seq'), parts along dimension 0, may hold values from -6 to 6
- attn_gate: float32 [1], replicated, may hold values from 0.3 to 1.5
- tile_count: int32 [8], P('group'), parts along dimension 0, may hold values from 1 to 4
- w_kv: bfloat16 [1280, 2048], replicated, may hold values from -0.15625 to 0.15625
- text_query: bfloat16 [4096, 6144], P(('group', 'seq')), parts along dimension 0, may hold values from -200 to 200
- text_image: int32 [4096], P(('group', 'seq')), parts along dimension 0, may hold values from 0 to 1, as said below
Outputs:
- vision_out: bfloat16 [8, 32, 1280], P('group', 'seq'), parts along dimension 0
- cross_out: bfloat16 [4096, 6144], P(('group', 'seq')), parts along dimension 0
The draws below stay inside these ranges and needn't reach their ends.
There are 4 independent parts, one for each index of `group`. The reference program is written for one: setup_inputs(seed, part) draws one part's arguments, and reference() takes and returns one part's arrays. A program takes and returns all parts, laid end to end along the dimension named above; an argument that names none is the same for every part. Nothing has to cross between parts.
Inputs may be any that keep to these rules, and one draw needn't show every extreme that they name: `text_image`: does not fall along the sequence; both values occur.
All inputs are finite; a program needn't handle non-finite values.
Results may differ from the reference program's by a relative error of at most 0.0035.
The reference program's roundings to bfloat16 on the way count: a program that leaves them out, or rounds other values in their place, can miss the bound.
Values may be sent and summed in bfloat16 or wider, within the bound.
A program may use at most 64 MiB of HBM per device.

```python
import math
import jax
import jax.numpy as jnp
from jax import lax

VHEADS = 16
KVH = 8
HD = 128
QGROUP = 6
IMAGES = 2
TILES = 4
VW = 1280
VIS = 32
TEXT = 1024


def vision_pair(key):
    first, second = jax.random.split(jax.random.fold_in(key, 11), 2)
    query = jax.random.normal(first, (IMAGES, VIS, VW), jnp.float32)
    keys = jax.random.normal(second, (IMAGES, VIS, VW), jnp.float32)
    query = jnp.clip(query, -6.0, 6.0)
    keys = jnp.clip(keys, -6.0, 6.0)
    return (query, keys)


def draw_vis_query(key, part):
    return vision_pair(key)[0].astype(jnp.bfloat16)


def draw_vis_key(key, part):
    return vision_pair(key)[1].astype(jnp.bfloat16)


def draw_text_query(key, part):
    first = jax.random.fold_in(jax.random.fold_in(key, 23), 0)
    values = jax.random.normal(first, (TEXT, KVH * QGROUP * HD), jnp.float32)
    values = jnp.clip(values, -6.0, 6.0)
    return values.astype(jnp.bfloat16)


def draw_text_image(key, part):
    border = jax.random.randint(jax.random.fold_in(key, 37), (), 1, TEXT)
    return (jnp.arange(TEXT, dtype=jnp.int32) >= border).astype(jnp.int32)


def levels(rng, shape, cuts, smallest, high):
    factor_of = 1.0
    for position, blocks in cuts:
        heights = jax.random.uniform(jax.random.fold_in(jax.random.fold_in(rng, 6), position), (blocks,), jnp.float32, smallest / len(cuts), high / len(cuts))
        factor_of = factor_of * jnp.repeat(jnp.exp(heights), shape[position] // blocks).reshape((-1,) + (1,) * (len(shape) - 1 - position))
    return factor_of


def gaussian(key, shape, spread, bound, cuts=(), held_as=jnp.bfloat16):
    factor_of = levels(key, shape, cuts, -0.22, 0.18) if cuts else 1.0
    entries = jax.random.normal(key, shape, jnp.float32) * spread * factor_of
    return jnp.minimum(jnp.maximum(entries, -bound), bound).astype(held_as)


def setup_inputs(seed: int = 0, part: int = 0) -> dict:
    splits = jax.random.split(jax.random.key(seed), 10)
    part_splits = jax.random.split(jax.random.fold_in(splits[9], part), 10)
    return {
        "vis_query": draw_vis_query(jax.random.fold_in(jax.random.fold_in(splits[9], part), 71), part),
        "vis_key": draw_vis_key(jax.random.fold_in(jax.random.fold_in(splits[9], part), 71), part),
        "vis_value": gaussian(part_splits[2], (IMAGES, VIS, VW), 1.0, 6.0, ((1, 8),)),
        "vis_resid": gaussian(part_splits[3], (IMAGES, VIS, VW), 1.0, 6.0, ((1, 8),)),
        "attn_gate": jnp.clip(jax.random.uniform(splits[4], (1,), jnp.float32, 0.3, 1.5), 0.3, 1.5),
        "tile_count": jax.random.randint(part_splits[5], (IMAGES,), 1, TILES + 1).astype(jnp.int32),
        "w_kv": gaussian(splits[6], (VW, 2 * KVH * HD), VW ** -0.5, 0.15625),
        "text_query": draw_text_query(jax.random.fold_in(jax.random.fold_in(splits[9], part), 71), part),
        "text_image": draw_text_image(jax.random.fold_in(jax.random.fold_in(splits[9], part), 71), part),
    }


def reference(vis_query, vis_key, vis_value, vis_resid, attn_gate, tile_count, w_kv, text_query, text_image):
    images, length, width = vis_query.shape
    hsize = width // VHEADS
    patch = length // TILES
    tile_of = jnp.arange(length, dtype=jnp.int32) // patch
    key_ok = tile_of[None, :] < tile_count[:, None]
    query = vis_query.astype(jnp.float32).reshape(images, length, VHEADS, hsize)
    keys = vis_key.astype(jnp.float32).reshape(images, length, VHEADS, hsize)
    values = vis_value.astype(jnp.float32).reshape(images, length, VHEADS, hsize)
    scores = jnp.einsum('bqhd,bkhd->bhqk', query, keys, precision=lax.Precision.HIGHEST) / math.sqrt(hsize)
    scores = jnp.where(key_ok[:, None, None, :], scores, -1e+30)
    peak = lax.optimization_barrier(jnp.max(scores, axis=-1, keepdims=True))
    expo = jnp.exp(scores - peak)
    probs = (expo / lax.optimization_barrier(jnp.sum(expo, axis=-1, keepdims=True))).astype(jnp.bfloat16)
    attn = jnp.einsum('bhqk,bkhd->bqhd', probs.astype(jnp.float32), values, precision=lax.Precision.HIGHEST)
    attn = attn.reshape(images, length, width)
    vision_out = (vis_resid.astype(jnp.float32) + jnp.tanh(attn_gate[0]) * attn).astype(jnp.bfloat16)
    cross_kv = jnp.dot(vision_out.reshape(images * length, width), w_kv, preferred_element_type=jnp.float32).astype(jnp.bfloat16)
    half = KVH * HD
    cross_key = cross_kv[:, :half].astype(jnp.float32).reshape(images * length, KVH, HD)
    cross_value = cross_kv[:, half:].astype(jnp.float32).reshape(images * length, KVH, HD)
    image_of_key = jnp.arange(images * length, dtype=jnp.int32) // length
    flat_ok = key_ok.reshape(images * length)
    total = text_query.shape[0]
    block = 512 if total % 512 == 0 else total
    count = total // block
    queries = text_query.reshape(count, block, KVH * QGROUP * HD)
    seen = text_image.reshape(count, block)

    def one_block(pair):
        rows, last = pair
        qrows = rows.astype(jnp.float32).reshape(block, KVH, QGROUP, HD)
        score = jnp.einsum('tgqd,kgd->tgqk', qrows, cross_key, precision=lax.Precision.HIGHEST) / math.sqrt(HD)
        allowed = (image_of_key[None, :] <= last[:, None]) & flat_ok[None, :]
        score = jnp.where(allowed[:, None, None, :], score, -1e+30)
        top = lax.optimization_barrier(jnp.max(score, axis=-1, keepdims=True))
        ex = jnp.exp(score - top)
        prob = (ex / lax.optimization_barrier(jnp.sum(ex, axis=-1, keepdims=True))).astype(jnp.bfloat16)
        out = jnp.einsum('tgqk,kgd->tgqd', prob.astype(jnp.float32), cross_value, precision=lax.Precision.HIGHEST)
        return out.reshape(block, KVH * QGROUP * HD).astype(jnp.bfloat16)
    cross_out = lax.map(one_block, (queries, seen)).reshape(total, KVH * QGROUP * HD)
    return (vision_out, cross_out)
```

```python
import functools
import math

import jax
import jax.numpy as jnp
from jax import lax
from jax.experimental import pallas as pl
from jax.experimental.pallas import tpu as pltpu
from jax.sharding import PartitionSpec as P

VHEADS = 16
VHEAD = 80
KVH = 8
HD = 128
QGROUP = 6
TILES = 4
LANES = 128
NEG = -1e30


def vision_attend(query, keys, values, tile_count, nheads):
    images, rows, width = query.shape
    length = keys.shape[1]
    patch = length // TILES
    tile_of = jnp.arange(length, dtype=jnp.int32) // patch
    key_ok = tile_of[None, :] < tile_count[:, None]
    query = query.reshape(images, rows, nheads, VHEAD)
    keys = keys.reshape(images, length, nheads, VHEAD)
    values = values.reshape(images, length, nheads, VHEAD)
    scores = jnp.einsum(
        "bqhd,bkhd->bhqk", query, keys, preferred_element_type=jnp.float32
    ) / math.sqrt(VHEAD)
    scores = jnp.where(key_ok[:, None, None, :], scores, NEG)
    peak = jnp.max(scores, axis=-1, keepdims=True)
    expo = jnp.exp(scores - peak)
    probs = (expo / jnp.sum(expo, axis=-1, keepdims=True)).astype(jnp.bfloat16)
    attn = jnp.einsum("bhqk,bkhd->bqhd", probs, values, preferred_element_type=jnp.float32)
    return attn.reshape(images, rows, width)


def general_form(
    vis_query, vis_key, vis_value, vis_resid, attn_gate, tile_count, w_kv, text_query, text_image
):
    images, rows, width = vis_query.shape
    keys, values = (
        lax.all_gather(vis_key, "seq", axis=1, tiled=True),
        lax.all_gather(vis_value, "seq", axis=1, tiled=True),
    )
    attn = vision_attend(vis_query, keys, values, tile_count, VHEADS)
    vision_out = (vis_resid.astype(jnp.float32) + jnp.tanh(attn_gate[0]) * attn).astype(
        jnp.bfloat16
    )
    local_kv = jnp.dot(
        vision_out.reshape(images * rows, width), w_kv, preferred_element_type=jnp.float32
    )
    local_kv = local_kv.astype(jnp.bfloat16).reshape(images, rows, w_kv.shape[1])
    cross_kv = lax.all_gather(local_kv, "seq", axis=1, tiled=True)
    length = cross_kv.shape[1]
    patch = length // TILES
    tile_of = jnp.arange(length, dtype=jnp.int32) // patch
    key_ok = tile_of[None, :] < tile_count[:, None]
    half = KVH * HD
    flat_kv = cross_kv.reshape(images * length, 2 * half)
    cross_key = flat_kv[:, :half].reshape(images * length, KVH, HD)
    cross_value = flat_kv[:, half:].reshape(images * length, KVH, HD)
    image_of_key = jnp.arange(images * length, dtype=jnp.int32) // length
    flat_ok = key_ok.reshape(images * length)
    tokens = text_query.shape[0]
    qrows = text_query.reshape(tokens, KVH, QGROUP, HD)
    score = jnp.einsum(
        "tgqd,kgd->tgqk", qrows, cross_key, preferred_element_type=jnp.float32
    ) / math.sqrt(HD)
    allowed = (image_of_key[None, :] <= text_image[:, None]) & flat_ok[None, :]
    score = jnp.where(allowed[:, None, None, :], score, NEG)
    top = jnp.max(score, axis=-1, keepdims=True)
    expd = jnp.exp(score - top)
    prob = (expd / jnp.sum(expd, axis=-1, keepdims=True)).astype(jnp.bfloat16)
    out = jnp.einsum("tgqk,kgd->tgqd", prob, cross_value, preferred_element_type=jnp.float32)
    cross_out = out.reshape(tokens, KVH * QGROUP * HD).astype(jnp.bfloat16)
    return (vision_out, cross_out)


def key_facts(index, images, rows, length, counts):
    image = (index // rows) % images
    place = (index // (images * rows)) * rows + index % rows
    tile = place // (length // TILES)
    count = jnp.zeros_like(index)
    for b in range(images):
        count = jnp.where(image == b, counts[b], count)
    return image, tile < count


def vision_kernel(
    n, images, rows, width,
    gate_ref, count_ref, q_in, k_in, v_in, r_in, w_in,
    out_ref, kv_ref,
    slots, stage, w_vmem, vis_all, load_sem, w_sem, send_sem, recv_sem,
):
    me = lax.axis_index("seq")
    chips = n // 2
    half = chips // 2
    chip, core = me // 2, me % 2
    partner = chip * 2 + (1 - core)
    block = images * rows
    total = n * block

    w_copy = pltpu.make_async_copy(w_in, w_vmem, w_sem)
    loads = [
        pltpu.make_async_copy(ref, slots.at[me, a], load_sem.at[a])
        for a, ref in enumerate((q_in, k_in, v_in, r_in))
    ]
    for load in loads:
        load.start()

    peers = []
    for ky in reversed(range(half)):
        for kx in reversed(range(2)):
            if ky or kx:
                there = ((chip // 2 + ky) % half) * 2 + (chip % 2 + kx) % 2
                peers.append((there * 2 + core, there * 2 + (1 - core)))

    def signal(dev, sem):
        pl.semaphore_signal(
            sem, inc=1, device_id={"seq": dev}, device_id_type=pl.DeviceIdType.MESH
        )

    barrier = pltpu.get_barrier_semaphore()
    for dev, _ in peers:
        signal(dev, barrier)
    signal(partner, barrier)
    w_copy.start()
    pl.semaphore_wait(barrier, len(peers) + 1)
    for load in loads:
        load.wait()

    def send(slot, dev, number):
        return pltpu.make_async_remote_copy(
            src_ref=slots.at[slot],
            dst_ref=slots.at[slot],
            send_sem=send_sem.at[number],
            recv_sem=recv_sem.at[slot],
            device_id={"seq": dev},
            device_id_type=pl.DeviceIdType.MESH,
        )

    sent = [send(me, dev, i) for i, (dev, _) in enumerate(peers)]
    sent.append(send(me, partner, len(peers)))
    for copy in sent:
        copy.start()

    def unpack(slot):
        at = pl.multiple_of(slot * block, block)
        for a in range(4):
            pieces = [slots[slot, a, b].astype(jnp.float32) for b in range(images)]
            stage[a, pl.ds(at, block), :] = jnp.concatenate(pieces, axis=0)

    def arrived(slot):
        send(slot, partner, 0).wait_recv()

    unpack(me)
    arrived(partner)
    unpack(partner)
    for i, (dev, _) in reversed(list(enumerate(peers))):
        arrived(dev)
        relay = send(dev, partner, len(peers) + 1 + i)
        relay.start()
        sent.append(relay)
        unpack(dev)
    for dev, other in reversed(peers):
        arrived(other)
        unpack(other)

    length = n * rows
    counts = [count_ref[b] for b in range(images)]
    k_index = lax.broadcasted_iota(jnp.int32, (total, total), 1)
    q_index = lax.broadcasted_iota(jnp.int32, (total, total), 0)
    k_image, k_ok = key_facts(k_index, images, rows, length, counts)
    q_image = (q_index // rows) % images
    ok = (k_image == q_image) & k_ok
    heads = width // VHEAD
    query = stage[0].astype(jnp.bfloat16)
    key = stage[1].astype(jnp.bfloat16)
    value = stage[2].astype(jnp.bfloat16)
    parts = [None] * (width // LANES)
    for h in range(heads):
        first, last = h * VHEAD, (h + 1) * VHEAD
        t0, t1 = first // LANES, -(-last // LANES)
        lo, hi = t0 * LANES, t1 * LANES
        lane = lax.broadcasted_iota(jnp.int32, (total, hi - lo), 1) + lo
        mine = (lane >= first) & (lane < last)
        zero = jnp.zeros((), jnp.bfloat16)
        k_h = jnp.where(mine, key[:, lo:hi], zero)
        v_h = jnp.where(mine, value[:, lo:hi], zero)
        score = lax.dot_general(
            query[:, lo:hi], k_h, (((1,), (1,)), ((), ())), preferred_element_type=jnp.float32
        ) / math.sqrt(VHEAD)
        score = jnp.where(ok, score, NEG)
        expo = jnp.exp(score - jnp.max(score, axis=-1, keepdims=True))
        prob = (expo / jnp.sum(expo, axis=-1, keepdims=True)).astype(jnp.bfloat16)
        attn = jnp.dot(prob, v_h, preferred_element_type=jnp.float32)
        for t in range(t0, t1):
            piece = attn[:, (t - t0) * LANES : (t - t0 + 1) * LANES]
            parts[t] = piece if parts[t] is None else parts[t] + piece
    gate = jnp.tanh(jnp.full((1, LANES), gate_ref[0], jnp.float32))
    for t, part in enumerate(parts):
        cols = slice(t * LANES, (t + 1) * LANES)
        vis_all[:, cols] = stage[3, :, cols] + gate * part
    mine = vis_all[pl.ds(pl.multiple_of(me * block, block), block), :]
    for b in range(images):
        out_ref[b] = mine[b * rows : (b + 1) * rows].astype(jnp.bfloat16)
    vis = vis_all[...].astype(jnp.bfloat16)
    w_copy.wait()
    step = 2 * LANES
    for j in range(w_vmem.shape[1] // step):
        cols = slice(j * step, (j + 1) * step)
        kv_ref[:, cols] = jnp.dot(
            vis, w_vmem[:, cols], preferred_element_type=jnp.float32
        ).astype(jnp.bfloat16)
    for copy in sent:
        copy.wait_send()


def vision_part(n, q, k, v, r, gate, count, w_kv):
    images, rows, width = q.shape
    total = n * images * rows
    anyspace = pl.BlockSpec(memory_space=pl.ANY)
    smem = pl.BlockSpec(memory_space=pltpu.SMEM)
    vmem = pl.BlockSpec(memory_space=pltpu.VMEM)
    return pl.pallas_call(
        functools.partial(vision_kernel, n, images, rows, width),
        out_shape=(
            jax.ShapeDtypeStruct(q.shape, jnp.bfloat16),
            jax.ShapeDtypeStruct((total, w_kv.shape[1]), jnp.bfloat16),
        ),
        in_specs=[smem, smem] + [anyspace] * 5,
        out_specs=(vmem, vmem),
        scratch_shapes=[
            pltpu.VMEM((n, 4, images, rows, width), jnp.bfloat16),
            pltpu.VMEM((4, total, width), jnp.float32),
            pltpu.VMEM(w_kv.shape, jnp.bfloat16),
            pltpu.VMEM((total, width), jnp.float32),
            pltpu.SemaphoreType.DMA((4,)),
            pltpu.SemaphoreType.DMA,
            pltpu.SemaphoreType.DMA((n,)),
            pltpu.SemaphoreType.DMA((n,)),
        ],
        compiler_params=pltpu.CompilerParams(collective_id=0, has_side_effects=True),
        name="vision",
    )(gate, count, q, k, v, r, w_kv)


def text_kernel(
    images, rows, length, groups,
    count_ref, seen_ref, vis_ref, q_ref, k_ref, v_ref, vis_out, o_ref, allow_ref,
):
    tokens = q_ref.shape[0]
    keys = images * length

    @pl.when(pl.program_id(0) == 0)
    def _():
        vis_out[...] = vis_ref[...]
        counts = [count_ref[b] for b in range(images)]
        index = lax.broadcasted_iota(jnp.int32, (tokens, LANES), 1) % keys
        token = lax.broadcasted_iota(jnp.int32, (tokens, LANES), 0)
        image, ok = key_facts(index, images, rows, length, counts)
        seen = seen_ref[...]
        border = jnp.zeros_like(token)
        for b in range(1, images):
            below = jnp.sum((seen < b).astype(jnp.float32), axis=-1, keepdims=True)
            border = jnp.where(image == b, below.astype(jnp.int32), border)
        allow_ref[...] = (ok & (token >= border)).astype(jnp.float32)

    allowed = allow_ref[...] > 0.5
    left = lax.broadcasted_iota(jnp.int32, (tokens, LANES), 1) < keys
    for g in range(groups):
        k_g = k_ref[:, g * HD : (g + 1) * HD]
        v_g = v_ref[:, g * HD : (g + 1) * HD]
        zero = jnp.zeros_like(k_g)
        k_two = jnp.concatenate(
            [jnp.concatenate([k_g, zero], axis=1), jnp.concatenate([zero, k_g], axis=1)], axis=0
        )
        v_two = jnp.concatenate(
            [jnp.concatenate([v_g, zero], axis=1), jnp.concatenate([zero, v_g], axis=1)], axis=0
        )
        for j in range(QGROUP // 2):
            cols = slice((g * QGROUP + 2 * j) * HD, (g * QGROUP + 2 * j + 2) * HD)
            score = lax.dot_general(
                q_ref[:, cols], k_two, (((1,), (1,)), ((), ())),
                preferred_element_type=jnp.float32,
            ) / math.sqrt(HD)
            score = jnp.where(allowed, score, NEG)
            low = jnp.finfo(jnp.float32).min
            top_l = jnp.max(jnp.where(left, score, low), axis=-1, keepdims=True)
            top_r = jnp.max(jnp.where(left, low, score), axis=-1, keepdims=True)
            expd = jnp.exp(score - jnp.where(left, top_l, top_r))
            sum_l = jnp.sum(jnp.where(left, expd, 0.0), axis=-1, keepdims=True)
            sum_r = jnp.sum(jnp.where(left, 0.0, expd), axis=-1, keepdims=True)
            prob = (expd / jnp.where(left, sum_l, sum_r)).astype(jnp.bfloat16)
            o_ref[:, cols] = jnp.dot(
                prob, v_two, preferred_element_type=jnp.float32
            ).astype(jnp.bfloat16)


def text_part(n, rows, count, seen, vis, query, kv):
    images = vis.shape[0]
    length = n * rows
    tokens = query.shape[0]
    groups = 2
    steps = KVH // groups
    smem = pl.BlockSpec(memory_space=pltpu.SMEM)
    vmem = pl.BlockSpec(memory_space=pltpu.VMEM)
    span = groups * QGROUP * HD
    return pl.pallas_call(
        functools.partial(text_kernel, images, rows, length, groups),
        grid=(steps,),
        out_shape=(
            jax.ShapeDtypeStruct(vis.shape, jnp.bfloat16),
            jax.ShapeDtypeStruct(query.shape, jnp.bfloat16),
        ),
        in_specs=[
            smem,
            vmem,
            vmem,
            pl.BlockSpec((tokens, span), lambda i: (0, i)),
            pl.BlockSpec((images * length, groups * HD), lambda i: (0, i)),
            pl.BlockSpec((images * length, groups * HD), lambda i: (0, i + steps)),
        ],
        out_specs=(vmem, pl.BlockSpec((tokens, span), lambda i: (0, i))),
        scratch_shapes=[pltpu.VMEM((tokens, LANES), jnp.float32)],
        name="text",
    )(count, seen.reshape(1, tokens), vis, query, kv, kv)


def on_device(n, *args):
    vis_query, vis_key, vis_value, vis_resid, attn_gate, tile_count, w_kv, text_query, text_image = args
    images, rows, width = vis_query.shape
    if n % 4 or 2 * images * rows * n != LANES or (images * rows) % 8:
        return general_form(*args)
    vis, kv = vision_part(
        n, vis_query, vis_key, vis_value, vis_resid, attn_gate, tile_count, w_kv
    )
    return text_part(n, rows, tile_count, text_image, vis, text_query, kv)


def solution(mesh):
    placed = (
        P("group", "seq", None),
        P("group", "seq", None),
        P("group", "seq", None),
        P("group", "seq", None),
        P(),
        P("group"),
        P(),
        P(("group", "seq"), None),
        P(("group", "seq")),
    )
    return jax.shard_map(
        functools.partial(on_device, mesh.shape["seq"]),
        mesh=mesh,
        in_specs=placed,
        out_specs=(P("group", "seq", None), P(("group", "seq"), None)),
        check_vma=False,
    )
```

```python
import functools
import math

import jax
import jax.numpy as jnp
from jax import lax
from jax.experimental import pallas as pl
from jax.experimental.pallas import tpu as pltpu
from jax.sharding import PartitionSpec as P

VHEADS = 16
VHEAD = 80
KVH = 8
HD = 128
QGROUP = 6
TILES = 4
LANES = 128
NEG = -1e30


def vision_attend(query, keys, values, tile_count, nheads):
    images, rows, width = query.shape
    length = keys.shape[1]
    patch = length // TILES
    tile_of = jnp.arange(length, dtype=jnp.int32) // patch
    key_ok = tile_of[None, :] < tile_count[:, None]
    query = query.reshape(images, rows, nheads, VHEAD)
    keys = keys.reshape(images, length, nheads, VHEAD)
    values = values.reshape(images, length, nheads, VHEAD)
    scores = jnp.einsum(
        "bqhd,bkhd->bhqk", query, keys, preferred_element_type=jnp.float32
    ) / math.sqrt(VHEAD)
    scores = jnp.where(key_ok[:, None, None, :], scores, NEG)
    peak = jnp.max(scores, axis=-1, keepdims=True)
    expo = jnp.exp(scores - peak)
    probs = (expo / jnp.sum(expo, axis=-1, keepdims=True)).astype(jnp.bfloat16)
    attn = jnp.einsum("bhqk,bkhd->bqhd", probs, values, preferred_element_type=jnp.float32)
    return attn.reshape(images, rows, width)


def general_form(
    vis_query, vis_key, vis_value, vis_resid, attn_gate, tile_count, w_kv, text_query, text_image
):
    images, rows, width = vis_query.shape
    keys, values = (
        lax.all_gather(vis_key, "seq", axis=1, tiled=True),
        lax.all_gather(vis_value, "seq", axis=1, tiled=True),
    )
    attn = vision_attend(vis_query, keys, values, tile_count, VHEADS)
    vision_out = (vis_resid.astype(jnp.float32) + jnp.tanh(attn_gate[0]) * attn).astype(
        jnp.bfloat16
    )
    local_kv = jnp.dot(
        vision_out.reshape(images * rows, width), w_kv, preferred_element_type=jnp.float32
    )
    local_kv = local_kv.astype(jnp.bfloat16).reshape(images, rows, w_kv.shape[1])
    cross_kv = lax.all_gather(local_kv, "seq", axis=1, tiled=True)
    length = cross_kv.shape[1]
    patch = length // TILES
    tile_of = jnp.arange(length, dtype=jnp.int32) // patch
    key_ok = tile_of[None, :] < tile_count[:, None]
    half = KVH * HD
    flat_kv = cross_kv.reshape(images * length, 2 * half)
    cross_key = flat_kv[:, :half].reshape(images * length, KVH, HD)
    cross_value = flat_kv[:, half:].reshape(images * length, KVH, HD)
    image_of_key = jnp.arange(images * length, dtype=jnp.int32) // length
    flat_ok = key_ok.reshape(images * length)
    tokens = text_query.shape[0]
    qrows = text_query.reshape(tokens, KVH, QGROUP, HD)
    score = jnp.einsum(
        "tgqd,kgd->tgqk", qrows, cross_key, preferred_element_type=jnp.float32
    ) / math.sqrt(HD)
    allowed = (image_of_key[None, :] <= text_image[:, None]) & flat_ok[None, :]
    score = jnp.where(allowed[:, None, None, :], score, NEG)
    top = jnp.max(score, axis=-1, keepdims=True)
    expd = jnp.exp(score - top)
    prob = (expd / jnp.sum(expd, axis=-1, keepdims=True)).astype(jnp.bfloat16)
    out = jnp.einsum("tgqk,kgd->tgqd", prob, cross_value, preferred_element_type=jnp.float32)
    cross_out = out.reshape(tokens, KVH * QGROUP * HD).astype(jnp.bfloat16)
    return (vision_out, cross_out)


GRANT = 16 * 1024 * 1024
MESH = pl.DeviceIdType.MESH


def spare_rows(images, rows):
    return -(-images * rows // 16) * 16


def vision_kernel(
    n, images, rows, width, tokens,
    gate_in, count_in, seen_in, q_in, k_in, v_in, r_in, w_in,
    pack_ref,
    slots, stage, w_vmem, vis_all, seen_ref, gate_ref, count_ref,
    load_sem, w_sem, small_sem, send_sem, recv_sem,
):
    me = lax.axis_index("seq")
    chips = n // 2
    half = chips // 2
    chip, core = me // 2, me % 2
    partner = chip * 2 + (1 - core)
    length = n * rows
    keys = images * length
    pair = 2 * rows

    loads = [
        pltpu.make_async_copy(ref.at[b], slots.at[me, b, a], load_sem.at[b, a])
        for b in range(images)
        for a, ref in enumerate((q_in, k_in, v_in, r_in))
    ]
    for load in loads:
        load.start()

    peers = []
    for ky in range(half):
        for kx in range(2):
            if ky or kx:
                there = ((chip // 2 + ky) % half) * 2 + (chip % 2 + kx) % 2
                peers.append((there, there * 2 + core, there * 2 + (1 - core)))

    barrier = pltpu.get_barrier_semaphore()
    for dev in [dev for _, dev, _ in peers] + [partner]:
        pl.semaphore_signal(barrier, inc=1, device_id={"seq": dev}, device_id_type=MESH)
    small = [
        pltpu.make_async_copy(gate_in, gate_ref, small_sem.at[0]),
        pltpu.make_async_copy(count_in, count_ref, small_sem.at[1]),
        pltpu.make_async_copy(seen_in, seen_ref, small_sem.at[2]),
    ]
    for copy in small:
        copy.start()
    w_copy = pltpu.make_async_copy(w_in, w_vmem, w_sem)
    w_copy.start()
    pl.semaphore_wait(barrier, len(peers) + 1)
    for load in loads:
        load.wait()

    def send(slot, b, dev, number):
        return pltpu.make_async_remote_copy(
            src_ref=slots.at[slot, b],
            dst_ref=slots.at[slot, b],
            send_sem=send_sem.at[b, number],
            recv_sem=recv_sem.at[b, slot],
            device_id={"seq": dev},
            device_id_type=MESH,
        )

    sent = []
    for b in range(images):
        for number, (_, dev, _) in reversed(list(enumerate(peers))):
            sent.append(send(me, b, dev, number))
        sent.append(send(me, b, partner, len(peers)))
    for copy in sent:
        copy.start()

    for copy in small:
        copy.wait()
    place = lax.broadcasted_iota(jnp.int32, (length, tokens), 0)
    kv_width = w_vmem.shape[1]
    for b in range(images):
        ok = (place // (length // TILES) < count_ref[b]) & (seen_ref[...] >= b)
        pack_ref[b * length : (b + 1) * length, kv_width : kv_width + tokens] = jnp.where(
            ok, 0.0, NEG
        ).astype(jnp.bfloat16)
    gate = jnp.tanh(jnp.full((1, LANES), gate_ref[0], jnp.float32))

    def arrived(slot, b):
        send(slot, b, partner, 0).wait_recv()

    def forward(b):
        for i, (_, dev, _) in enumerate(peers):
            arrived(dev, b)
            relay = send(dev, b, partner, len(peers) + 1 + i)
            relay.start()
            sent.append(relay)

    def unpack(there, b):
        at = pl.multiple_of(there * pair, pair)
        for a in range(4):
            two = [slots[there * 2 + c, b, a].astype(jnp.float32) for c in range(2)]
            stage[b, a, pl.ds(at, pair), :] = jnp.concatenate(two, axis=0)

    def gather(b):
        arrived(partner, b)
        unpack(chip, b)
        for there, _, other in peers:
            arrived(other, b)
            unpack(there, b)

    heads = width // VHEAD
    side = LANES // length
    key_row = lax.broadcasted_iota(jnp.int32, (length, LANES), 0)
    scale = math.log2(math.e) / math.sqrt(VHEAD)

    def attend(b):
        query = stage[b, 0].astype(jnp.bfloat16)
        key = stage[b, 1].astype(jnp.bfloat16)
        value = stage[b, 2].astype(jnp.bfloat16)
        bias = jnp.where(key_row // (length // TILES) < count_ref[b], 0.0, NEG)
        parts = [None] * (width // LANES)
        for h in range(0, heads, side):
            t0, t1 = h * VHEAD // LANES, -(-(h + side) * VHEAD // LANES)
            lo, hi = t0 * LANES, t1 * LANES
            lane = lax.broadcasted_iota(jnp.int32, (length, hi - lo), 1) + lo
            own = [
                (lane >= i * VHEAD) & (lane < (i + 1) * VHEAD) for i in range(h, h + side)
            ]
            window = query[:, lo:hi]
            spread = jnp.concatenate(
                [jnp.where(mask, window, jnp.zeros_like(window)) for mask in own], axis=0
            )
            score = lax.dot_general(
                key[:, lo:hi], spread, (((1,), (1,)), ((), ())),
                preferred_element_type=jnp.float32,
            )
            score = score + bias
            expo = jnp.exp2((score - jnp.max(score, axis=0, keepdims=True)) * scale)
            prob = expo * (1.0 / jnp.sum(expo, axis=0, keepdims=True))
            attn = lax.dot_general(
                prob.astype(jnp.bfloat16), value[:, lo:hi], (((0,), (0,)), ((), ())),
                preferred_element_type=jnp.float32,
            )
            total = jnp.zeros((length, hi - lo), jnp.float32)
            for i, mask in enumerate(own):
                total = jnp.where(mask, attn[i * length : (i + 1) * length], total)
            for t in range(t0, t1):
                piece = total[:, (t - t0) * LANES : (t - t0 + 1) * LANES]
                parts[t] = piece if parts[t] is None else parts[t] + piece
        for t, part in enumerate(parts):
            cols = slice(t * LANES, (t + 1) * LANES)
            vis_all[b, :, cols] = stage[b, 3, :, cols] + gate * part

    def project(b):
        vis = vis_all[b].astype(jnp.bfloat16)
        step = 2 * LANES
        for j in range(w_vmem.shape[1] // step):
            cols = slice(j * step, (j + 1) * step)
            pack_ref[b * length : (b + 1) * length, cols] = jnp.dot(
                vis, w_vmem[:, cols], preferred_element_type=jnp.float32
            ).astype(jnp.bfloat16)

    forward(0)
    gather(0)
    attend(0)
    w_copy.wait()
    for b in range(1, images):
        forward(b)
        project(b - 1)
        gather(b)
        attend(b)
    project(images - 1)
    mine = []
    for b in range(images):
        near = vis_all[b, pl.ds(pl.multiple_of(chip * pair, pair), pair), :]
        mine.append(jnp.where(core == 0, near[:rows], near[rows:]))
    mine.extend([jnp.zeros_like(mine[0])] * (spare_rows(images, rows) // rows - images))
    pack_ref[keys:, :width] = jnp.concatenate(mine, axis=0).astype(jnp.bfloat16)
    for copy in sent:
        copy.wait_send()


def vision_part(n, q, k, v, r, gate, count, seen, w_kv):
    images, rows, width = q.shape
    length = n * rows
    keys = images * length
    tokens = seen.shape[0]
    anyspace = pl.BlockSpec(memory_space=pltpu.HBM)
    vmem = pl.BlockSpec(memory_space=pltpu.VMEM)
    return pl.pallas_call(
        functools.partial(vision_kernel, n, images, rows, width, tokens),
        out_shape=jax.ShapeDtypeStruct(
            (keys + spare_rows(images, rows), w_kv.shape[1] + tokens), jnp.bfloat16
        ),
        in_specs=[anyspace] * 8,
        out_specs=vmem,
        scratch_shapes=[
            pltpu.VMEM((n, images, 4, rows, width), jnp.bfloat16),
            pltpu.VMEM((images, 4, length, width), jnp.float32),
            pltpu.VMEM(w_kv.shape, jnp.bfloat16),
            pltpu.VMEM((images, length, width), jnp.float32),
            pltpu.VMEM((1, tokens), jnp.int32),
            pltpu.SMEM((1,), jnp.float32),
            pltpu.SMEM((images,), jnp.int32),
            pltpu.SemaphoreType.DMA((images, 4)),
            pltpu.SemaphoreType.DMA,
            pltpu.SemaphoreType.DMA((3,)),
            pltpu.SemaphoreType.DMA((images, n)),
            pltpu.SemaphoreType.DMA((images, n)),
        ],
        compiler_params=pltpu.CompilerParams(
            collective_id=0, has_side_effects=True
        ),
        name="vision",
    )(gate, count, seen.reshape(1, tokens), q, k, v, r, w_kv)


def text_kernel(pack_ref, q_ref, vis_out, out_hbm, o_ref, bias_ref, out_sem):
    images, rows, width = vis_out.shape
    keys, tokens = bias_ref.shape[0] // 2, bias_ref.shape[1]
    for b in range(images):
        vis_out[b] = pack_ref[keys + b * rows : keys + (b + 1) * rows, :width]
    for twin in range(2):
        bias_ref[twin * keys : (twin + 1) * keys, :] = pack_ref[
            :keys, 2 * KVH * HD : 2 * KVH * HD + tokens
        ].astype(jnp.float32)
    scale = math.log2(math.e) / math.sqrt(HD)
    span = QGROUP * HD
    copies = []
    for g in range(KVH):
        k_g = pack_ref[:keys, g * HD : (g + 1) * HD]
        v_g = pack_ref[:keys, (KVH + g) * HD : (KVH + g + 1) * HD]
        zero = jnp.zeros_like(k_g)
        k_two = jnp.concatenate(
            [jnp.concatenate([k_g, zero], axis=1), jnp.concatenate([zero, k_g], axis=1)], axis=0
        )
        v_two = jnp.concatenate(
            [jnp.concatenate([v_g, zero], axis=1), jnp.concatenate([zero, v_g], axis=1)], axis=0
        )
        for j in range(QGROUP // 2):
            cols = slice(g * span + 2 * j * HD, g * span + (2 * j + 2) * HD)
            score = lax.dot_general(
                k_two, q_ref[:, cols], (((1,), (1,)), ((), ())),
                preferred_element_type=jnp.float32,
            )
            score = score + bias_ref[...]
            probs = []
            for part in (score[:keys], score[keys:]):
                expd = jnp.exp2((part - jnp.max(part, axis=0, keepdims=True)) * scale)
                probs.append(expd * (1.0 / jnp.sum(expd, axis=0, keepdims=True)))
            prob = jnp.concatenate(probs, axis=0).astype(jnp.bfloat16)
            o_ref[:, cols] = lax.dot_general(
                prob, v_two, (((0,), (0,)), ((), ())), preferred_element_type=jnp.float32
            ).astype(jnp.bfloat16)
        cols = pl.ds(g * span, span)
        copies.append(
            pltpu.make_async_copy(o_ref.at[:, cols], out_hbm.at[:, cols], out_sem.at[g])
        )
        copies[-1].start()
    for copy in copies:
        copy.wait()


def text_part(shape, keys, pack, query):
    vmem = pl.BlockSpec(memory_space=pltpu.VMEM)
    return pl.pallas_call(
        text_kernel,
        out_shape=(
            jax.ShapeDtypeStruct(shape, jnp.bfloat16),
            jax.ShapeDtypeStruct(query.shape, jnp.bfloat16),
        ),
        in_specs=[vmem] * 2,
        out_specs=(vmem, pl.BlockSpec(memory_space=pl.ANY)),
        scratch_shapes=[
            pltpu.VMEM(query.shape, jnp.bfloat16),
            pltpu.VMEM((2 * keys, query.shape[0]), jnp.float32),
            pltpu.SemaphoreType.DMA((KVH,)),
        ],
        compiler_params=pltpu.CompilerParams(vmem_limit_bytes=GRANT),
        name="text",
    )(pack, query)


def fits(n, images, rows, width):
    length = n * rows
    return (
        n % 4 == 0
        and 2 * images * length == LANES
        and LANES % length == 0
        and (width // VHEAD) % (LANES // length) == 0
        and (2 * rows) % 8 == 0
        and length % 16 == 0
        and spare_rows(images, rows) % rows == 0
    )


def on_device(n, *args):
    vis_query, vis_key, vis_value, vis_resid, attn_gate, tile_count, w_kv, text_query, text_image = args
    images, rows, width = vis_query.shape
    if not fits(n, images, rows, width):
        return general_form(*args)
    pack = vision_part(
        n, vis_query, vis_key, vis_value, vis_resid, attn_gate, tile_count, text_image, w_kv
    )
    return text_part(vis_query.shape, images * rows * n, pack, text_query)


def solution(mesh):
    placed = (
        P("group", "seq", None),
        P("group", "seq", None),
        P("group", "seq", None),
        P("group", "seq", None),
        P(),
        P("group"),
        P(),
        P(("group", "seq"), None),
        P(("group", "seq")),
    )
    return jax.shard_map(
        functools.partial(on_device, mesh.shape["seq"]),
        mesh=mesh,
        in_specs=placed,
        out_specs=(P("group", "seq", None), P(("group", "seq"), None)),
        check_vma=False,
    )
```

```python
import functools
import math

import jax
import jax.numpy as jnp
from jax import lax
from jax.experimental import pallas as pl
from jax.experimental.pallas import tpu as pltpu
from jax.sharding import PartitionSpec as P

VHEADS = 16
VHEAD = 80
KVH = 8
HD = 128
QGROUP = 6
TILES = 4
LANES = 128
NEG = -1e30


def vision_attend(query, keys, values, tile_count, nheads):
    images, rows, width = query.shape
    length = keys.shape[1]
    patch = length // TILES
    tile_of = jnp.arange(length, dtype=jnp.int32) // patch
    key_ok = tile_of[None, :] < tile_count[:, None]
    query = query.reshape(images, rows, nheads, VHEAD)
    keys = keys.reshape(images, length, nheads, VHEAD)
    values = values.reshape(images, length, nheads, VHEAD)
    scores = jnp.einsum(
        "bqhd,bkhd->bhqk", query, keys, preferred_element_type=jnp.float32
    ) / math.sqrt(VHEAD)
    scores = jnp.where(key_ok[:, None, None, :], scores, NEG)
    peak = jnp.max(scores, axis=-1, keepdims=True)
    expo = jnp.exp(scores - peak)
    probs = (expo / jnp.sum(expo, axis=-1, keepdims=True)).astype(jnp.bfloat16)
    attn = jnp.einsum("bhqk,bkhd->bqhd", probs, values, preferred_element_type=jnp.float32)
    return attn.reshape(images, rows, width)


def general_form(
    vis_query, vis_key, vis_value, vis_resid, attn_gate, tile_count, w_kv, text_query, text_image
):
    images, rows, width = vis_query.shape
    keys, values = (
        lax.all_gather(vis_key, "seq", axis=1, tiled=True),
        lax.all_gather(vis_value, "seq", axis=1, tiled=True),
    )
    attn = vision_attend(vis_query, keys, values, tile_count, VHEADS)
    vision_out = (vis_resid.astype(jnp.float32) + jnp.tanh(attn_gate[0]) * attn).astype(
        jnp.bfloat16
    )
    local_kv = jnp.dot(
        vision_out.reshape(images * rows, width), w_kv, preferred_element_type=jnp.float32
    )
    local_kv = local_kv.astype(jnp.bfloat16).reshape(images, rows, w_kv.shape[1])
    cross_kv = lax.all_gather(local_kv, "seq", axis=1, tiled=True)
    length = cross_kv.shape[1]
    patch = length // TILES
    tile_of = jnp.arange(length, dtype=jnp.int32) // patch
    key_ok = tile_of[None, :] < tile_count[:, None]
    half = KVH * HD
    flat_kv = cross_kv.reshape(images * length, 2 * half)
    cross_key = flat_kv[:, :half].reshape(images * length, KVH, HD)
    cross_value = flat_kv[:, half:].reshape(images * length, KVH, HD)
    image_of_key = jnp.arange(images * length, dtype=jnp.int32) // length
    flat_ok = key_ok.reshape(images * length)
    tokens = text_query.shape[0]
    qrows = text_query.reshape(tokens, KVH, QGROUP, HD)
    score = jnp.einsum(
        "tgqd,kgd->tgqk", qrows, cross_key, preferred_element_type=jnp.float32
    ) / math.sqrt(HD)
    allowed = (image_of_key[None, :] <= text_image[:, None]) & flat_ok[None, :]
    score = jnp.where(allowed[:, None, None, :], score, NEG)
    top = jnp.max(score, axis=-1, keepdims=True)
    expd = jnp.exp(score - top)
    prob = (expd / jnp.sum(expd, axis=-1, keepdims=True)).astype(jnp.bfloat16)
    out = jnp.einsum("tgqk,kgd->tgqd", prob, cross_value, preferred_element_type=jnp.float32)
    cross_out = out.reshape(tokens, KVH * QGROUP * HD).astype(jnp.bfloat16)
    return (vision_out, cross_out)


GRANT = 16 * 1024 * 1024
MESH = pl.DeviceIdType.MESH


def spare_rows(images, rows):
    return -(-images * rows // 16) * 16


def vision_kernel(
    n, images, rows, width, tokens,
    gate_in, count_in, seen_in, q_in, k_in, v_in, r_in, w_in,
    pack_hbm,
    pack_ref, slots, stage, w_vmem, vis_all, seen_ref, gate_ref, count_ref,
    load_sem, w_sem, small_sem, send_sem, recv_sem, out_sem,
):
    me = lax.axis_index("seq")
    chips = n // 2
    half = chips // 2
    chip, core = me // 2, me % 2
    partner = chip * 2 + (1 - core)
    length = n * rows
    keys = images * length
    pair = 2 * rows

    loads = [
        pltpu.make_async_copy(ref.at[b], slots.at[me, b, a], load_sem.at[b, a])
        for b in range(images)
        for a, ref in enumerate((q_in, k_in, v_in, r_in))
    ]
    for load in loads:
        load.start()

    peers = []
    for ky in range(half):
        for kx in range(2):
            if ky or kx:
                there = ((chip // 2 + ky) % half) * 2 + (chip % 2 + kx) % 2
                peers.append((there, there * 2 + core, there * 2 + (1 - core)))

    barrier = pltpu.get_barrier_semaphore()
    for dev in [dev for _, dev, _ in peers] + [partner]:
        pl.semaphore_signal(barrier, inc=1, device_id={"seq": dev}, device_id_type=MESH)
    small = [
        pltpu.make_async_copy(gate_in, gate_ref, small_sem.at[0]),
        pltpu.make_async_copy(count_in, count_ref, small_sem.at[1]),
        pltpu.make_async_copy(seen_in, seen_ref, small_sem.at[2]),
    ]
    for copy in small:
        copy.start()
    w_copy = pltpu.make_async_copy(w_in, w_vmem, w_sem)
    w_copy.start()
    pl.semaphore_wait(barrier, len(peers) + 1)
    for load in loads:
        load.wait()

    def send(slot, b, dev, number):
        return pltpu.make_async_remote_copy(
            src_ref=slots.at[slot, b],
            dst_ref=slots.at[slot, b],
            send_sem=send_sem.at[b, number],
            recv_sem=recv_sem.at[b, slot],
            device_id={"seq": dev},
            device_id_type=MESH,
        )

    sent = []
    for b in range(images):
        for number, (_, dev, _) in reversed(list(enumerate(peers))):
            sent.append(send(me, b, dev, number))
        sent.append(send(me, b, partner, len(peers)))
    for copy in sent:
        copy.start()

    for copy in small:
        copy.wait()
    place = lax.broadcasted_iota(jnp.int32, (length, tokens), 0)
    kv_width = w_vmem.shape[1]
    for b in range(images):
        ok = (place // (length // TILES) < count_ref[b]) & (seen_ref[...] >= b)
        pack_ref[b * length : (b + 1) * length, kv_width : kv_width + tokens] = jnp.where(
            ok, 0.0, NEG
        ).astype(jnp.bfloat16)
    out = []

    def write(at_rows, at_cols):
        copy = pltpu.make_async_copy(
            pack_ref.at[at_rows, at_cols], pack_hbm.at[at_rows, at_cols], out_sem.at[len(out)]
        )
        copy.start()
        out.append(copy)

    write(pl.ds(0, keys), pl.ds(kv_width, tokens))
    gate = jnp.tanh(jnp.full((1, LANES), gate_ref[0], jnp.float32))

    def arrived(slot, b):
        send(slot, b, partner, 0).wait_recv()

    def forward(b):
        for i, (_, dev, _) in enumerate(peers):
            arrived(dev, b)
            relay = send(dev, b, partner, len(peers) + 1 + i)
            relay.start()
            sent.append(relay)

    def unpack(there, b):
        at = pl.multiple_of(there * pair, pair)
        for a in range(4):
            two = [slots[there * 2 + c, b, a].astype(jnp.float32) for c in range(2)]
            stage[b, a, pl.ds(at, pair), :] = jnp.concatenate(two, axis=0)

    def gather(b):
        arrived(partner, b)
        unpack(chip, b)
        for there, _, other in peers:
            arrived(other, b)
            unpack(there, b)

    heads = width // VHEAD
    side = LANES // length
    key_row = lax.broadcasted_iota(jnp.int32, (length, LANES), 0)
    scale = math.log2(math.e) / math.sqrt(VHEAD)

    def attend(b):
        query = stage[b, 0].astype(jnp.bfloat16)
        key = stage[b, 1].astype(jnp.bfloat16)
        value = stage[b, 2].astype(jnp.bfloat16)
        bias = jnp.where(key_row // (length // TILES) < count_ref[b], 0.0, NEG)
        parts = [None] * (width // LANES)
        for h in range(0, heads, side):
            t0, t1 = h * VHEAD // LANES, -(-(h + side) * VHEAD // LANES)
            lo, hi = t0 * LANES, t1 * LANES
            lane = lax.broadcasted_iota(jnp.int32, (length, hi - lo), 1) + lo
            own = [
                (lane >= i * VHEAD) & (lane < (i + 1) * VHEAD) for i in range(h, h + side)
            ]
            window = query[:, lo:hi]
            spread = jnp.concatenate(
                [jnp.where(mask, window, jnp.zeros_like(window)) for mask in own], axis=0
            )
            score = lax.dot_general(
                key[:, lo:hi], spread, (((1,), (1,)), ((), ())),
                preferred_element_type=jnp.float32,
            )
            score = score + bias
            expo = jnp.exp2((score - jnp.max(score, axis=0, keepdims=True)) * scale)
            prob = expo * (1.0 / jnp.sum(expo, axis=0, keepdims=True))
            attn = lax.dot_general(
                prob.astype(jnp.bfloat16), value[:, lo:hi], (((0,), (0,)), ((), ())),
                preferred_element_type=jnp.float32,
            )
            total = jnp.zeros((length, hi - lo), jnp.float32)
            for i, mask in enumerate(own):
                total = jnp.where(mask, attn[i * length : (i + 1) * length], total)
            for t in range(t0, t1):
                piece = total[:, (t - t0) * LANES : (t - t0 + 1) * LANES]
                parts[t] = piece if parts[t] is None else parts[t] + piece
        for t, part in enumerate(parts):
            cols = slice(t * LANES, (t + 1) * LANES)
            vis_all[b, :, cols] = stage[b, 3, :, cols] + gate * part

    def project(b):
        vis = vis_all[b].astype(jnp.bfloat16)
        step = 2 * LANES
        for j in range(w_vmem.shape[1] // step):
            cols = slice(j * step, (j + 1) * step)
            pack_ref[b * length : (b + 1) * length, cols] = jnp.dot(
                vis, w_vmem[:, cols], preferred_element_type=jnp.float32
            ).astype(jnp.bfloat16)
            if b == images - 1:
                write(pl.ds(0, keys), pl.ds(j * step, step))

    forward(0)
    gather(0)
    attend(0)
    w_copy.wait()
    for b in range(1, images):
        forward(b)
        project(b - 1)
        gather(b)
        attend(b)
    mine = []
    for b in range(images):
        near = vis_all[b, pl.ds(pl.multiple_of(chip * pair, pair), pair), :]
        mine.append(jnp.where(core == 0, near[:rows], near[rows:]))
    mine.extend([jnp.zeros_like(mine[0])] * (spare_rows(images, rows) // rows - images))
    pack_ref[keys:, :width] = jnp.concatenate(mine, axis=0).astype(jnp.bfloat16)
    write(pl.ds(keys, spare_rows(images, rows)), pl.ds(0, width))
    project(images - 1)
    for copy in out:
        copy.wait()
    for copy in sent:
        copy.wait_send()


def vision_part(n, q, k, v, r, gate, count, seen, w_kv):
    images, rows, width = q.shape
    length = n * rows
    keys = images * length
    tokens = seen.shape[0]
    anyspace = pl.BlockSpec(memory_space=pltpu.HBM)
    return pl.pallas_call(
        functools.partial(vision_kernel, n, images, rows, width, tokens),
        out_shape=jax.ShapeDtypeStruct(
            (keys + spare_rows(images, rows), w_kv.shape[1] + tokens), jnp.bfloat16
        ),
        in_specs=[anyspace] * 8,
        out_specs=anyspace,
        scratch_shapes=[
            pltpu.VMEM((keys + spare_rows(images, rows), w_kv.shape[1] + tokens), jnp.bfloat16),
            pltpu.VMEM((n, images, 4, rows, width), jnp.bfloat16),
            pltpu.VMEM((images, 4, length, width), jnp.float32),
            pltpu.VMEM(w_kv.shape, jnp.bfloat16),
            pltpu.VMEM((images, length, width), jnp.float32),
            pltpu.VMEM((1, tokens), jnp.int32),
            pltpu.SMEM((1,), jnp.float32),
            pltpu.SMEM((images,), jnp.int32),
            pltpu.SemaphoreType.DMA((images, 4)),
            pltpu.SemaphoreType.DMA,
            pltpu.SemaphoreType.DMA((3,)),
            pltpu.SemaphoreType.DMA((images, n)),
            pltpu.SemaphoreType.DMA((images, n)),
            pltpu.SemaphoreType.DMA((2 + w_kv.shape[1] // (2 * LANES),)),
        ],
        compiler_params=pltpu.CompilerParams(
            collective_id=0, has_side_effects=True
        ),
        name="vision",
    )(gate, count, seen.reshape(1, tokens), q, k, v, r, w_kv)


def text_kernel(pack_ref, q_ref, vis_out, out_hbm, o_ref, bias_ref, out_sem):
    images, rows, width = vis_out.shape
    keys, tokens = bias_ref.shape[0] // 2, bias_ref.shape[1]
    for b in range(images):
        vis_out[b] = pack_ref[keys + b * rows : keys + (b + 1) * rows, :width]
    for twin in range(2):
        bias_ref[twin * keys : (twin + 1) * keys, :] = pack_ref[
            :keys, 2 * KVH * HD : 2 * KVH * HD + tokens
        ].astype(jnp.float32)
    scale = math.log2(math.e) / math.sqrt(HD)
    span = QGROUP * HD
    copies = []
    for g in range(KVH):
        k_g = pack_ref[:keys, g * HD : (g + 1) * HD]
        v_g = pack_ref[:keys, (KVH + g) * HD : (KVH + g + 1) * HD]
        zero = jnp.zeros_like(k_g)
        k_two = jnp.concatenate(
            [jnp.concatenate([k_g, zero], axis=1), jnp.concatenate([zero, k_g], axis=1)], axis=0
        )
        v_two = jnp.concatenate(
            [jnp.concatenate([v_g, zero], axis=1), jnp.concatenate([zero, v_g], axis=1)], axis=0
        )
        for j in range(QGROUP // 2):
            cols = slice(g * span + 2 * j * HD, g * span + (2 * j + 2) * HD)
            score = lax.dot_general(
                k_two, q_ref[:, cols], (((1,), (1,)), ((), ())),
                preferred_element_type=jnp.float32,
            )
            score = score + bias_ref[...]
            probs = []
            for part in (score[:keys], score[keys:]):
                expd = jnp.exp2((part - jnp.max(part, axis=0, keepdims=True)) * scale)
                probs.append(expd * (1.0 / jnp.sum(expd, axis=0, keepdims=True)))
            prob = jnp.concatenate(probs, axis=0).astype(jnp.bfloat16)
            o_ref[:, cols] = lax.dot_general(
                prob, v_two, (((0,), (0,)), ((), ())), preferred_element_type=jnp.float32
            ).astype(jnp.bfloat16)
        cols = pl.ds(g * span, span)
        copies.append(
            pltpu.make_async_copy(o_ref.at[:, cols], out_hbm.at[:, cols], out_sem.at[g])
        )
        copies[-1].start()
    for copy in copies:
        copy.wait()


def text_part(shape, keys, pack, query):
    vmem = pl.BlockSpec(memory_space=pltpu.VMEM)
    return pl.pallas_call(
        text_kernel,
        out_shape=(
            jax.ShapeDtypeStruct(shape, jnp.bfloat16),
            jax.ShapeDtypeStruct(query.shape, jnp.bfloat16),
        ),
        in_specs=[vmem] * 2,
        out_specs=(vmem, pl.BlockSpec(memory_space=pl.ANY)),
        scratch_shapes=[
            pltpu.VMEM(query.shape, jnp.bfloat16),
            pltpu.VMEM((2 * keys, query.shape[0]), jnp.float32),
            pltpu.SemaphoreType.DMA((KVH,)),
        ],
        compiler_params=pltpu.CompilerParams(vmem_limit_bytes=GRANT),
        name="text",
    )(pack, query)


def fits(n, images, rows, width):
    length = n * rows
    return (
        n % 4 == 0
        and 2 * images * length == LANES
        and LANES % length == 0
        and (width // VHEAD) % (LANES // length) == 0
        and (2 * rows) % 8 == 0
        and length % 16 == 0
        and spare_rows(images, rows) % rows == 0
    )


def on_device(n, *args):
    vis_query, vis_key, vis_value, vis_resid, attn_gate, tile_count, w_kv, text_query, text_image = args
    images, rows, width = vis_query.shape
    if not fits(n, images, rows, width):
        return general_form(*args)
    pack = vision_part(
        n, vis_query, vis_key, vis_value, vis_resid, attn_gate, tile_count, text_image, w_kv
    )
    return text_part(vis_query.shape, images * rows * n, pack, text_query)


def solution(mesh):
    placed = (
        P("group", "seq", None),
        P("group", "seq", None),
        P("group", "seq", None),
        P("group", "seq", None),
        P(),
        P("group"),
        P(),
        P(("group", "seq"), None),
        P(("group", "seq")),
    )
    return jax.shard_map(
        functools.partial(on_device, mesh.shape["seq"]),
        mesh=mesh,
        in_specs=placed,
        out_specs=(P("group", "seq", None), P(("group", "seq"), None)),
        check_vma=False,
    )
```

```python
import functools
import math

import jax
import jax.numpy as jnp
from jax import lax
from jax.experimental import pallas as pl
from jax.experimental.pallas import tpu as pltpu
from jax.sharding import PartitionSpec as P

VHEADS = 16
VHEAD = 80
KVH = 8
HD = 128
QGROUP = 6
TILES = 4
LANES = 128
NEG = -1e30


def vision_attend(query, keys, values, tile_count, nheads):
    images, rows, width = query.shape
    length = keys.shape[1]
    patch = length // TILES
    tile_of = jnp.arange(length, dtype=jnp.int32) // patch
    key_ok = tile_of[None, :] < tile_count[:, None]
    query = query.reshape(images, rows, nheads, VHEAD)
    keys = keys.reshape(images, length, nheads, VHEAD)
    values = values.reshape(images, length, nheads, VHEAD)
    scores = jnp.einsum(
        "bqhd,bkhd->bhqk", query, keys, preferred_element_type=jnp.float32
    ) / math.sqrt(VHEAD)
    scores = jnp.where(key_ok[:, None, None, :], scores, NEG)
    peak = jnp.max(scores, axis=-1, keepdims=True)
    expo = jnp.exp(scores - peak)
    probs = (expo / jnp.sum(expo, axis=-1, keepdims=True)).astype(jnp.bfloat16)
    attn = jnp.einsum("bhqk,bkhd->bqhd", probs, values, preferred_element_type=jnp.float32)
    return attn.reshape(images, rows, width)


def general_form(
    vis_query, vis_key, vis_value, vis_resid, attn_gate, tile_count, w_kv, text_query, text_image
):
    images, rows, width = vis_query.shape
    keys, values = (
        lax.all_gather(vis_key, "seq", axis=1, tiled=True),
        lax.all_gather(vis_value, "seq", axis=1, tiled=True),
    )
    attn = vision_attend(vis_query, keys, values, tile_count, VHEADS)
    vision_out = (vis_resid.astype(jnp.float32) + jnp.tanh(attn_gate[0]) * attn).astype(
        jnp.bfloat16
    )
    local_kv = jnp.dot(
        vision_out.reshape(images * rows, width), w_kv, preferred_element_type=jnp.float32
    )
    local_kv = local_kv.astype(jnp.bfloat16).reshape(images, rows, w_kv.shape[1])
    cross_kv = lax.all_gather(local_kv, "seq", axis=1, tiled=True)
    length = cross_kv.shape[1]
    patch = length // TILES
    tile_of = jnp.arange(length, dtype=jnp.int32) // patch
    key_ok = tile_of[None, :] < tile_count[:, None]
    half = KVH * HD
    flat_kv = cross_kv.reshape(images * length, 2 * half)
    cross_key = flat_kv[:, :half].reshape(images * length, KVH, HD)
    cross_value = flat_kv[:, half:].reshape(images * length, KVH, HD)
    image_of_key = jnp.arange(images * length, dtype=jnp.int32) // length
    flat_ok = key_ok.reshape(images * length)
    tokens = text_query.shape[0]
    qrows = text_query.reshape(tokens, KVH, QGROUP, HD)
    score = jnp.einsum(
        "tgqd,kgd->tgqk", qrows, cross_key, preferred_element_type=jnp.float32
    ) / math.sqrt(HD)
    allowed = (image_of_key[None, :] <= text_image[:, None]) & flat_ok[None, :]
    score = jnp.where(allowed[:, None, None, :], score, NEG)
    top = jnp.max(score, axis=-1, keepdims=True)
    expd = jnp.exp(score - top)
    prob = (expd / jnp.sum(expd, axis=-1, keepdims=True)).astype(jnp.bfloat16)
    out = jnp.einsum("tgqk,kgd->tgqd", prob, cross_value, preferred_element_type=jnp.float32)
    cross_out = out.reshape(tokens, KVH * QGROUP * HD).astype(jnp.bfloat16)
    return (vision_out, cross_out)


GRANT = 16 * 1024 * 1024
MESH = pl.DeviceIdType.MESH


def spare_rows(images, rows):
    return -(-images * rows // 16) * 16


def vision_kernel(
    n, images, rows, width, tokens,
    gate_in, count_in, seen_in, q_in, k_in, v_in, r_in, w_in,
    pack_ref,
    slots, stage, w_vmem, vis_all, seen_ref, gate_ref, count_ref,
    load_sem, w_sem, small_sem, send_sem, recv_sem,
):
    me = lax.axis_index("seq")
    chips = n // 2
    half = chips // 2
    chip, core = me // 2, me % 2
    partner = chip * 2 + (1 - core)
    length = n * rows
    keys = images * length
    pair = 2 * rows

    loads = [
        pltpu.make_async_copy(ref.at[b], slots.at[me, b, a], load_sem.at[b, a])
        for b in range(images)
        for a, ref in enumerate((q_in, k_in, v_in, r_in))
    ]
    peers = []
    for ky in range(half):
        for kx in range(2):
            if ky or kx:
                there = ((chip // 2 + ky) % half) * 2 + (chip % 2 + kx) % 2
                peers.append((there, there * 2 + core, there * 2 + (1 - core)))

    barrier = pltpu.get_barrier_semaphore()
    for dev in [dev for _, dev, _ in peers] + [partner]:
        pl.semaphore_signal(barrier, inc=1, device_id={"seq": dev}, device_id_type=MESH)
    for load in loads:
        load.start()
    small = [
        pltpu.make_async_copy(gate_in, gate_ref, small_sem.at[0]),
        pltpu.make_async_copy(count_in, count_ref, small_sem.at[1]),
        pltpu.make_async_copy(seen_in, seen_ref, small_sem.at[2]),
    ]
    for copy in small:
        copy.start()
    w_copy = pltpu.make_async_copy(w_in, w_vmem, w_sem)
    w_copy.start()
    pl.semaphore_wait(barrier, len(peers) + 1)
    for load in loads:
        load.wait()

    def send(slot, b, dev, number):
        return pltpu.make_async_remote_copy(
            src_ref=slots.at[slot, b],
            dst_ref=slots.at[slot, b],
            send_sem=send_sem.at[b, number],
            recv_sem=recv_sem.at[b, slot],
            device_id={"seq": dev},
            device_id_type=MESH,
        )

    sent = []
    for b in range(images):
        for number, (_, dev, _) in reversed(list(enumerate(peers))):
            sent.append(send(me, b, dev, number))
        sent.append(send(me, b, partner, len(peers)))
    for copy in sent:
        copy.start()

    for copy in small:
        copy.wait()
    place = lax.broadcasted_iota(jnp.int32, (length, tokens), 0)
    kv_width = w_vmem.shape[1]
    for b in range(images):
        ok = (place // (length // TILES) < count_ref[b]) & (seen_ref[...] >= b)
        pack_ref[b * length : (b + 1) * length, kv_width : kv_width + tokens] = jnp.where(
            ok, 0.0, NEG
        ).astype(jnp.bfloat16)
    gate = jnp.tanh(jnp.full((1, LANES), gate_ref[0], jnp.float32))

    def arrived(slot, b):
        send(slot, b, partner, 0).wait_recv()

    def forward(b):
        for i, (_, dev, _) in enumerate(peers):
            arrived(dev, b)
            relay = send(dev, b, partner, len(peers) + 1 + i)
            relay.start()
            sent.append(relay)

    def unpack(there, b):
        at = pl.multiple_of(there * pair, pair)
        for a in range(4):
            two = [slots[there * 2 + c, b, a].astype(jnp.float32) for c in range(2)]
            stage[b, a, pl.ds(at, pair), :] = jnp.concatenate(two, axis=0)

    def gather(b):
        arrived(partner, b)
        unpack(chip, b)
        for there, _, other in peers:
            arrived(other, b)
            unpack(there, b)

    heads = width // VHEAD
    side = LANES // length
    key_row = lax.broadcasted_iota(jnp.int32, (length, LANES), 0)
    scale = math.log2(math.e) / math.sqrt(VHEAD)

    def attend(b):
        query = stage[b, 0].astype(jnp.bfloat16)
        key = stage[b, 1].astype(jnp.bfloat16)
        value = stage[b, 2].astype(jnp.bfloat16)
        bias = jnp.where(key_row // (length // TILES) < count_ref[b], 0.0, NEG)
        parts = [None] * (width // LANES)
        for h in range(0, heads, side):
            t0, t1 = h * VHEAD // LANES, -(-(h + side) * VHEAD // LANES)
            lo, hi = t0 * LANES, t1 * LANES
            lane = lax.broadcasted_iota(jnp.int32, (length, hi - lo), 1) + lo
            own = [
                (lane >= i * VHEAD) & (lane < (i + 1) * VHEAD) for i in range(h, h + side)
            ]
            window = query[:, lo:hi]
            spread = jnp.concatenate(
                [jnp.where(mask, window, jnp.zeros_like(window)) for mask in own], axis=0
            )
            score = lax.dot_general(
                key[:, lo:hi], spread, (((1,), (1,)), ((), ())),
                preferred_element_type=jnp.float32,
            )
            score = score + bias
            expo = jnp.exp2((score - jnp.max(score, axis=0, keepdims=True)) * scale)
            prob = expo * (1.0 / jnp.sum(expo, axis=0, keepdims=True))
            attn = lax.dot_general(
                prob.astype(jnp.bfloat16), value[:, lo:hi], (((0,), (0,)), ((), ())),
                preferred_element_type=jnp.float32,
            )
            total = jnp.zeros((length, hi - lo), jnp.float32)
            for i, mask in enumerate(own):
                total = jnp.where(mask, attn[i * length : (i + 1) * length], total)
            for t in range(t0, t1):
                piece = total[:, (t - t0) * LANES : (t - t0 + 1) * LANES]
                parts[t] = piece if parts[t] is None else parts[t] + piece
        for t, part in enumerate(parts):
            cols = slice(t * LANES, (t + 1) * LANES)
            vis_all[b, :, cols] = stage[b, 3, :, cols] + gate * part

    def project(b):
        vis = vis_all[b].astype(jnp.bfloat16)
        step = 2 * LANES
        for j in range(w_vmem.shape[1] // step):
            cols = slice(j * step, (j + 1) * step)
            pack_ref[b * length : (b + 1) * length, cols] = jnp.dot(
                vis, w_vmem[:, cols], preferred_element_type=jnp.float32
            ).astype(jnp.bfloat16)

    forward(0)
    gather(0)
    attend(0)
    w_copy.wait()
    for b in range(1, images):
        forward(b)
        project(b - 1)
        gather(b)
        attend(b)
    project(images - 1)
    mine = []
    for b in range(images):
        near = vis_all[b, pl.ds(pl.multiple_of(chip * pair, pair), pair), :]
        mine.append(jnp.where(core == 0, near[:rows], near[rows:]))
    mine.extend([jnp.zeros_like(mine[0])] * (spare_rows(images, rows) // rows - images))
    pack_ref[keys:, :width] = jnp.concatenate(mine, axis=0).astype(jnp.bfloat16)
    for copy in sent:
        copy.wait_send()


def vision_part(n, q, k, v, r, gate, count, seen, w_kv):
    images, rows, width = q.shape
    length = n * rows
    keys = images * length
    tokens = seen.shape[0]
    anyspace = pl.BlockSpec(memory_space=pltpu.HBM)
    vmem = pl.BlockSpec(memory_space=pltpu.VMEM)
    return pl.pallas_call(
        functools.partial(vision_kernel, n, images, rows, width, tokens),
        out_shape=jax.ShapeDtypeStruct(
            (keys + spare_rows(images, rows), w_kv.shape[1] + tokens), jnp.bfloat16
        ),
        in_specs=[anyspace] * 8,
        out_specs=vmem,
        scratch_shapes=[
            pltpu.VMEM((n, images, 4, rows, width), jnp.bfloat16),
            pltpu.VMEM((images, 4, length, width), jnp.float32),
            pltpu.VMEM(w_kv.shape, jnp.bfloat16),
            pltpu.VMEM((images, length, width), jnp.float32),
            pltpu.VMEM((1, tokens), jnp.int32),
            pltpu.SMEM((1,), jnp.float32),
            pltpu.SMEM((images,), jnp.int32),
            pltpu.SemaphoreType.DMA((images, 4)),
            pltpu.SemaphoreType.DMA,
            pltpu.SemaphoreType.DMA((3,)),
            pltpu.SemaphoreType.DMA((images, n)),
            pltpu.SemaphoreType.DMA((images, n)),
        ],
        compiler_params=pltpu.CompilerParams(
            collective_id=0, has_side_effects=True
        ),
        name="vision",
    )(gate, count, seen.reshape(1, tokens), q, k, v, r, w_kv)


def text_kernel(pack_ref, q_ref, vis_out, out_hbm, o_ref, bias_ref, out_sem):
    images, rows, width = vis_out.shape
    keys, tokens = bias_ref.shape[0] // 2, bias_ref.shape[1]
    for b in range(images):
        vis_out[b] = pack_ref[keys + b * rows : keys + (b + 1) * rows, :width]
    for twin in range(2):
        bias_ref[twin * keys : (twin + 1) * keys, :] = pack_ref[
            :keys, 2 * KVH * HD : 2 * KVH * HD + tokens
        ].astype(jnp.float32)
    scale = math.log2(math.e) / math.sqrt(HD)
    span = QGROUP * HD
    copies = []
    for g in range(KVH):
        k_g = pack_ref[:keys, g * HD : (g + 1) * HD]
        v_g = pack_ref[:keys, (KVH + g) * HD : (KVH + g + 1) * HD]
        zero = jnp.zeros_like(k_g)
        k_two = jnp.concatenate(
            [jnp.concatenate([k_g, zero], axis=1), jnp.concatenate([zero, k_g], axis=1)], axis=0
        )
        v_two = jnp.concatenate(
            [jnp.concatenate([v_g, zero], axis=1), jnp.concatenate([zero, v_g], axis=1)], axis=0
        )
        for j in range(QGROUP // 2):
            cols = slice(g * span + 2 * j * HD, g * span + (2 * j + 2) * HD)
            score = lax.dot_general(
                k_two, q_ref[:, cols], (((1,), (1,)), ((), ())),
                preferred_element_type=jnp.float32,
            )
            score = score + bias_ref[...]
            probs = []
            for part in (score[:keys], score[keys:]):
                expd = jnp.exp2((part - jnp.max(part, axis=0, keepdims=True)) * scale)
                probs.append(expd * (1.0 / jnp.sum(expd, axis=0, keepdims=True)))
            prob = jnp.concatenate(probs, axis=0).astype(jnp.bfloat16)
            o_ref[:, cols] = lax.dot_general(
                prob, v_two, (((0,), (0,)), ((), ())), preferred_element_type=jnp.float32
            ).astype(jnp.bfloat16)
        cols = pl.ds(g * span, span)
        copies.append(
            pltpu.make_async_copy(o_ref.at[:, cols], out_hbm.at[:, cols], out_sem.at[g])
        )
        copies[-1].start()
    for copy in copies:
        copy.wait()


def text_part(shape, keys, pack, query):
    vmem = pl.BlockSpec(memory_space=pltpu.VMEM)
    return pl.pallas_call(
        text_kernel,
        out_shape=(
            jax.ShapeDtypeStruct(shape, jnp.bfloat16),
            jax.ShapeDtypeStruct(query.shape, jnp.bfloat16),
        ),
        in_specs=[vmem] * 2,
        out_specs=(vmem, pl.BlockSpec(memory_space=pl.ANY)),
        scratch_shapes=[
            pltpu.VMEM(query.shape, jnp.bfloat16),
            pltpu.VMEM((2 * keys, query.shape[0]), jnp.float32),
            pltpu.SemaphoreType.DMA((KVH,)),
        ],
        compiler_params=pltpu.CompilerParams(vmem_limit_bytes=GRANT),
        name="text",
    )(pack, query)


def fits(n, images, rows, width):
    length = n * rows
    return (
        n % 4 == 0
        and 2 * images * length == LANES
        and LANES % length == 0
        and (width // VHEAD) % (LANES // length) == 0
        and (2 * rows) % 8 == 0
        and length % 16 == 0
        and spare_rows(images, rows) % rows == 0
    )


def on_device(n, *args):
    vis_query, vis_key, vis_value, vis_resid, attn_gate, tile_count, w_kv, text_query, text_image = args
    images, rows, width = vis_query.shape
    if not fits(n, images, rows, width):
        return general_form(*args)
    pack = vision_part(
        n, vis_query, vis_key, vis_value, vis_resid, attn_gate, tile_count, text_image, w_kv
    )
    return text_part(vis_query.shape, images * rows * n, pack, text_query)


def solution(mesh):
    placed = (
        P("group", "seq", None),
        P("group", "seq", None),
        P("group", "seq", None),
        P("group", "seq", None),
        P(),
        P("group"),
        P(),
        P(("group", "seq"), None),
        P(("group", "seq")),
    )
    return jax.shard_map(
        functools.partial(on_device, mesh.shape["seq"]),
        mesh=mesh,
        in_specs=placed,
        out_specs=(P("group", "seq", None), P(("group", "seq"), None)),
        check_vma=False,
    )
```
